512 devices in a mesh: seq: 16 (over y, x), head: 32 (over z, core).
Axes of the slice: x: 4, y: 4, z: 16, core: 2. Of those that a mesh axis runs over, the one named last changes fastest.
Arguments:
- query: bfloat16 [65536, 8192], P(('seq', 'head')), may hold values from -10 to 10
- sampled_key_value: bfloat16 [2, 65536, 1024], P(None, ('seq', 'head')), may hold values from -6 to 6
- cached_prompt_key_value: bfloat16 [2, 1024, 1024], P(None, 'seq'), may hold values from -6 to 6
- ancestor_block: int32 [512], replicated, may hold values from -1 to 511, as said below
Outputs:
- attended: bfloat16 [65536, 8192], P(('seq', 'head'))
The draws below stay inside these ranges and needn't reach their ends.
Inputs may be any that keep to these rules, and one draw needn't show every extreme that they name: `ancestor_block`: A block whose entry is not -1 has a parent whose own entry is -1. Groups are aligned runs of 32 blocks; half the blocks of every group have a parent, and for every pair of groups the number of blocks of the one whose parent lies in the other is either 0 or exactly 2.
All inputs are finite; a program needn't handle non-finite values.
Results may differ from the reference program's by a relative error of at most 0.0049.
Values may be sent and summed in bfloat16 or wider, within the bound.
A program may use at most 64 MiB of HBM per device.

```python
import math
import jax
import jax.numpy as jnp
from jax import lax

QUERY_HEADS = 64
KEY_VALUE_HEADS = 8
HEAD_SIZE = 128
TREE_BLOCK_SIZE = 128
PROMPT_TOKENS = 1024
CAP = 2
BLK_GRP = 32
NBLK = 512
SAMPLED_TOKENS = 65536


def draw_query(key, part):
    random_root_key = jax.random.fold_in(key, 11)
    drawn_value_rows = jnp.clip(jax.random.normal(random_root_key, (SAMPLED_TOKENS, QUERY_HEADS * HEAD_SIZE), jnp.float32), -6.0, 6.0)
    return drawn_value_rows.astype(jnp.bfloat16)


def draw_cached_prompt_key_value(key, part):
    random_root_key = jax.random.fold_in(key, 13)
    drawn_value_rows = jnp.clip(jax.random.normal(random_root_key, (2, PROMPT_TOKENS, KEY_VALUE_HEADS * HEAD_SIZE), jnp.float32), -6.0, 6.0)
    return drawn_value_rows.astype(jnp.bfloat16)


def draw_ancestor_block(key, part):
    group_count = NBLK // BLK_GRP
    half_blocks = BLK_GRP // 2
    perm_keys = jax.random.split(jax.random.fold_in(key, 1), group_count)
    rest = jax.vmap(lambda one_key: jax.random.permutation(one_key, BLK_GRP - 1))(perm_keys).astype(jnp.int32)
    last_col = jnp.full((group_count, 1), BLK_GRP - 1, jnp.int32)
    orders = jnp.concatenate([rest[:, :half_blocks], last_col, rest[:, half_blocks:]], axis=1)
    offset_keys = jax.random.split(jax.random.fold_in(key, 2), group_count)
    offsets = jax.vmap(lambda one_key: jax.random.permutation(one_key, group_count)[:half_blocks // CAP])(offset_keys).astype(jnp.int32)
    first_row = offsets[0]
    first_value = first_row[0]
    first_row = jnp.where(first_row == group_count - 1, first_value, first_row)
    first_row = first_row.at[0].set(group_count - 1)
    offsets = offsets.at[0].set(first_row)
    child_index = jnp.arange(half_blocks, dtype=jnp.int32)
    sources = (jnp.arange(group_count, dtype=jnp.int32)[:, None] + offsets[:, child_index // CAP]) % group_count
    choose = jax.random.randint(jax.random.fold_in(key, 3), (group_count, half_blocks), 0, half_blocks).astype(jnp.int32)
    choose = choose.at[0, 0].set(0)
    parent_ids = sources * BLK_GRP + orders[sources, half_blocks + choose]
    positions = jnp.arange(group_count, dtype=jnp.int32)[:, None] * BLK_GRP + orders[:, :half_blocks]
    result = jnp.full((NBLK,), -1, jnp.int32)
    return result.at[positions.reshape(-1)].set(parent_ids.reshape(-1).astype(jnp.int32))


def levels(rng, extent, cuts, smallest, high):
    def one(dim, blocks):
        heights = jax.random.uniform(jax.random.fold_in(jax.random.fold_in(rng, 6), dim), (blocks,), jnp.float32, smallest / len(cuts), high / len(cuts))
        return jnp.repeat(jnp.exp(heights), extent[dim] // blocks).reshape((-1,) + (1,) * (len(extent) - dim - 1))

    gain = one(*cuts[0])
    for cut in cuts[1:]:
        gain = gain * one(*cut)
    return gain


def scatter_about(rng, dims, scale, reach, shards=(), kind=jnp.bfloat16):
    values = scale * jax.random.normal(rng, dims, jnp.float32)
    if shards:
        values = values * levels(rng, dims, shards, -0.22, 0.18)
    return jnp.clip(values, -reach, reach).astype(kind)


def setup_inputs(seed: int = 0) -> dict:
    splits = jax.random.split(jax.random.key(seed), 5)
    query = draw_query(jax.random.fold_in(splits[4], 71), 0)
    sampled_key_value = scatter_about(splits[1], (2, SAMPLED_TOKENS, KEY_VALUE_HEADS * HEAD_SIZE), 1.0, 6.0, ((1, 512),))
    cached_prompt_key_value = draw_cached_prompt_key_value(jax.random.fold_in(splits[4], 71), 0)
    ancestor_block = draw_ancestor_block(jax.random.fold_in(splits[4], 71), 0)
    return {"query": query, "sampled_key_value": sampled_key_value, "cached_prompt_key_value": cached_prompt_key_value, "ancestor_block": ancestor_block}


def reference(query, sampled_key_value, cached_prompt_key_value, ancestor_block):
    tree_blocks = query.shape[0] // TREE_BLOCK_SIZE
    query_per_key_ratio = QUERY_HEADS // KEY_VALUE_HEADS
    inv_root = 1.0 / math.sqrt(HEAD_SIZE)
    query_rows = query.reshape(tree_blocks, TREE_BLOCK_SIZE, KEY_VALUE_HEADS, query_per_key_ratio, HEAD_SIZE)
    block_pairs = sampled_key_value.reshape(2, tree_blocks, TREE_BLOCK_SIZE, KEY_VALUE_HEADS, HEAD_SIZE)
    cached_prompt_keys = cached_prompt_key_value[0].reshape(PROMPT_TOKENS, KEY_VALUE_HEADS, HEAD_SIZE).astype(jnp.float32)
    cached_prompt_values = cached_prompt_key_value[1].reshape(PROMPT_TOKENS, KEY_VALUE_HEADS, HEAD_SIZE).astype(jnp.float32)
    causal = jnp.arange(TREE_BLOCK_SIZE, dtype=jnp.int32)[:, None] >= jnp.arange(TREE_BLOCK_SIZE, dtype=jnp.int32)[None, :]

    def one_block(block_index):
        parent = ancestor_block[block_index]
        has_parent = parent >= 0
        safe_parent = jnp.maximum(parent, 0).astype(jnp.int32)
        all_keys = jnp.concatenate([cached_prompt_keys, block_pairs[0, block_index].astype(jnp.float32), block_pairs[0, safe_parent].astype(jnp.float32)], axis=0)
        all_values = jnp.concatenate([cached_prompt_values, block_pairs[1, block_index].astype(jnp.float32), block_pairs[1, safe_parent].astype(jnp.float32)], axis=0)
        scores = jnp.einsum('qjrd,kjd->jrqk', query_rows[block_index].astype(jnp.float32), all_keys) * inv_root
        visible = jnp.concatenate([jnp.ones((TREE_BLOCK_SIZE, PROMPT_TOKENS), bool), causal, jnp.broadcast_to(has_parent, (TREE_BLOCK_SIZE, TREE_BLOCK_SIZE))], axis=1)
        scores = jnp.where(visible, scores, -jnp.inf)
        row_peak = lax.optimization_barrier(jnp.max(scores, axis=3, keepdims=True))
        shifted = jnp.exp(scores - row_peak)
        row_total = lax.optimization_barrier(jnp.sum(shifted, axis=3, keepdims=True))
        weights = (shifted / row_total).astype(jnp.bfloat16)
        result = jnp.einsum('jrqk,kjd->qjrd', weights.astype(jnp.float32), all_values)
        return result.astype(jnp.bfloat16).reshape(TREE_BLOCK_SIZE, QUERY_HEADS * HEAD_SIZE)
    outputs = lax.map(one_block, jnp.arange(tree_blocks, dtype=jnp.int32))
    return outputs.reshape(tree_blocks * TREE_BLOCK_SIZE, QUERY_HEADS * HEAD_SIZE)
```

```python
import functools
import math

import jax
import jax.numpy as jnp
from jax import lax
from jax.experimental import pallas as pl
from jax.experimental.pallas import tpu as pltpu
from jax.sharding import PartitionSpec as P

QUERY_HEADS = 64
KEY_VALUE_HEADS = 8
HEAD_SIZE = 128
BLOCK = 128
RATIO = QUERY_HEADS // KEY_VALUE_HEADS
CAP = 2
PIECE = 8
EXP2_SCALE = math.log2(math.e) / math.sqrt(HEAD_SIZE)


def dot(left, right, contract_right):
    return lax.dot_general(
        left, right, (((1,), (contract_right,)), ((), ())), preferred_element_type=jnp.float32
    )


def attention_kernel(parent_ref, q_ref, own_ref, prompt_ref, far_ref, o_ref, k_s, v_s, *, heads):
    prompt = prompt_ref.shape[1]
    total = prompt + 2 * BLOCK
    for target, source in ((k_s, 0), (v_s, 1)):
        target[0:prompt, 0:HEAD_SIZE] = prompt_ref[source]
        target[prompt : prompt + BLOCK, 0:HEAD_SIZE] = own_ref[source]
        target[prompt + BLOCK : total, 0:HEAD_SIZE] = far_ref[source]
    v_s[:, HEAD_SIZE:] = jnp.ones((total, HEAD_SIZE), jnp.bfloat16)
    has_parent = parent_ref[0] >= 0
    rows = heads * BLOCK
    row = lax.broadcasted_iota(jnp.int32, (rows, BLOCK), 0) % BLOCK
    col = lax.broadcasted_iota(jnp.int32, (rows, BLOCK), 1)
    causal = col <= row
    for step in range(RATIO // heads):
        spans = [
            slice((step * heads + i) * HEAD_SIZE, (step * heads + i + 1) * HEAD_SIZE)
            for i in range(heads)
        ]
        q = jnp.concatenate([q_ref[:, span] for span in spans], axis=0)
        scores = dot(q, k_s[...], 1)
        own = jnp.where(causal, scores[:, prompt : prompt + BLOCK], -jnp.inf)
        far = jnp.where(has_parent, scores[:, prompt + BLOCK :], -jnp.inf)
        scores = jnp.concatenate([scores[:, :prompt], own, far], axis=1)
        peak = jnp.max(scores, axis=1, keepdims=True)
        weights = jnp.exp2(scores * EXP2_SCALE - peak * EXP2_SCALE)
        summed = dot(weights.astype(jnp.bfloat16), v_s[...], 0)
        out = (summed[:, :HEAD_SIZE] / summed[:, HEAD_SIZE:]).astype(jnp.bfloat16)
        for i, span in enumerate(spans):
            o_ref[:, span] = out[i * BLOCK : (i + 1) * BLOCK]


def attention(parent, query, own, prompt, far):
    prompt_tokens = prompt.shape[1]
    total = prompt_tokens + 2 * BLOCK
    group = RATIO * HEAD_SIZE
    return pl.pallas_call(
        functools.partial(attention_kernel, heads=2),
        grid_spec=pltpu.PrefetchScalarGridSpec(
            num_scalar_prefetch=1,
            grid=(KEY_VALUE_HEADS,),
            in_specs=[
                pl.BlockSpec((BLOCK, group), lambda j, p: (0, j)),
                pl.BlockSpec((2, BLOCK, HEAD_SIZE), lambda j, p: (0, 0, j)),
                pl.BlockSpec((2, prompt_tokens, HEAD_SIZE), lambda j, p: (0, 0, j)),
                pl.BlockSpec((2, BLOCK, HEAD_SIZE), lambda j, p: (0, 0, j)),
            ],
            out_specs=pl.BlockSpec((BLOCK, group), lambda j, p: (0, j)),
            scratch_shapes=[
                pltpu.VMEM((total, HEAD_SIZE), jnp.bfloat16),
                pltpu.VMEM((total, 2 * HEAD_SIZE), jnp.bfloat16),
            ],
        ),
        out_shape=jax.ShapeDtypeStruct((BLOCK, QUERY_HEADS * HEAD_SIZE), jnp.bfloat16),
        compiler_params=pltpu.CompilerParams(vmem_limit_bytes=40 * 2**20),
        name="attention",
    )(parent, query, own, prompt, far)


def pick_kernel(index_ref, x_ref, o_ref):
    def step(i, carry):
        o_ref[i] = x_ref[index_ref[i]]
        return carry

    lax.fori_loop(0, o_ref.shape[0], step, 0)


def pick(index, x):
    return pl.pallas_call(
        pick_kernel,
        in_specs=[
            pl.BlockSpec(memory_space=pltpu.SMEM),
            pl.BlockSpec(memory_space=pltpu.VMEM),
        ],
        out_specs=pl.BlockSpec(memory_space=pltpu.VMEM),
        out_shape=jax.ShapeDtypeStruct((index.shape[0],) + x.shape[1:], x.dtype),
        name="pick",
    )(index, x)


def tables(ancestor_block, groups, blocks, group_index):
    parents = ancestor_block.reshape(groups, blocks)
    has_parent = parents >= 0
    source = jnp.where(has_parent, parents // blocks, -1)
    place = jnp.where(has_parent, parents % blocks, 0)
    iota = jnp.arange(blocks, dtype=jnp.int32)
    earlier = iota[None, :] < iota[:, None]
    same = (source[:, :, None] == source[:, None, :]) & has_parent[:, None, :] & earlier[None]
    rank = jnp.sum(same.astype(jnp.int32), axis=2)
    mine = source == group_index
    slots = jnp.arange(CAP, dtype=jnp.int32)
    hot = mine[:, None, :] & (rank[:, None, :] == slots[None, :, None])
    outgoing = jnp.sum(jnp.where(hot, place[:, None, :], 0), axis=2).reshape(groups * CAP)
    own_source = lax.dynamic_index_in_dim(source, group_index, 0, keepdims=False)
    own_rank = lax.dynamic_index_in_dim(rank, group_index, 0, keepdims=False)
    incoming = jnp.where(own_source >= 0, own_source * CAP + own_rank, 0)
    return outgoing, incoming


def body(query, sampled_key_value, cached_prompt_key_value, ancestor_block):
    groups = lax.axis_size("seq")
    blocks = lax.axis_size("head")
    group_index = lax.axis_index("seq")
    head_index = lax.axis_index("head")
    width = KEY_VALUE_HEADS * HEAD_SIZE
    outgoing, incoming = tables(ancestor_block, groups, blocks, group_index)
    parent = lax.dynamic_slice_in_dim(ancestor_block, group_index * blocks + head_index, 1, 0)
    prompt = lax.all_gather(cached_prompt_key_value, "seq", axis=1, tiled=True)
    pieces = sampled_key_value.reshape(blocks, PIECE, width)
    held = lax.all_to_all(pieces, "head", split_axis=0, concat_axis=0, tiled=True)
    sent = pick(outgoing, held)
    landed = lax.all_to_all(sent, "seq", split_axis=0, concat_axis=0, tiled=True)
    spread = pick(incoming, landed)
    far = lax.all_to_all(spread, "head", split_axis=0, concat_axis=0, tiled=True)
    far = far.reshape(2, BLOCK, width)
    return attention(parent, query, sampled_key_value, prompt, far)


def solution(mesh):
    placed = (P(("seq", "head"), None), P(None, ("seq", "head"), None), P(None, "seq", None), P())
    return jax.shard_map(
        body, mesh=mesh, in_specs=placed, out_specs=P(("seq", "head"), None), check_vma=False
    )
```

```python
import functools
import math

import jax
import jax.numpy as jnp
from jax import lax
from jax.experimental import pallas as pl
from jax.experimental.pallas import tpu as pltpu
from jax.sharding import PartitionSpec as P

QUERY_HEADS = 64
KEY_VALUE_HEADS = 8
HEAD_SIZE = 128
BLOCK = 128
RATIO = QUERY_HEADS // KEY_VALUE_HEADS
CAP = 2
WIDTH = KEY_VALUE_HEADS * HEAD_SIZE
PIECE_ROWS = 16
PIECE_COLS = WIDTH // 2
CHUNKS = 2
CHUNK_COLS = PIECE_COLS // CHUNKS
HALF = WIDTH // 2
HEADS = 2
EXP2_SCALE = math.log2(math.e) / math.sqrt(HEAD_SIZE)
MESH = pl.DeviceIdType.MESH


def dot(left, right, contract_right):
    return lax.dot_general(
        left, right, (((1,), (contract_right,)), ((), ())), preferred_element_type=jnp.float32
    )


def piece_of(ref, index, chunk):
    row = pl.multiple_of(((index // 2) % (BLOCK // PIECE_ROWS)) * PIECE_ROWS, PIECE_ROWS)
    col = pl.multiple_of((index % 2) * PIECE_COLS + chunk * CHUNK_COLS, CHUNK_COLS)
    kv = index // (2 * (BLOCK // PIECE_ROWS))
    return ref.at[kv, pl.ds(row, PIECE_ROWS), pl.ds(col, CHUNK_COLS)]


def kernel(
    groups,
    blocks,
    anc_ref,
    q_ref,
    own_ref,
    shard_ref,
    o_ref,
    prompt_0,
    prompt_1,
    held_0,
    held_1,
    sent_0,
    sent_1,
    landed_0,
    landed_1,
    spread_0,
    spread_1,
    far_0,
    far_1,
    k_s,
    v_s,
    acc_s,
    peak_s,
    out_tab,
    in_tab,
    held_send,
    held_recv,
    land_send,
    land_recv,
    far_send,
    far_recv,
    prompt_send,
    prompt_recv,
    pass_send,
    pass_recv,
    local_sem,
):
    held, sent = (held_0, held_1), (sent_0, sent_1)
    landed, spread = (landed_0, landed_1), (spread_0, spread_1)
    prompt, far = (prompt_0, prompt_1), (far_0, far_1)
    group = lax.axis_index("seq")
    place = lax.axis_index("head")
    core = place % 2
    twin = place + 1 - 2 * core
    shard_rows = shard_ref.shape[1]
    prompt_rows = groups * shard_rows

    barrier = pltpu.get_barrier_semaphore()

    def greet(axis, size, me):
        def step(k, carry):
            pl.semaphore_signal(
                barrier, inc=1, device_id={axis: (me + k) % size}, device_id_type=MESH
            )
            return carry

        lax.fori_loop(1, size, step, 0)

    greet("head", blocks, place)
    greet("seq", groups, group)

    own_pieces = [
        pltpu.make_async_copy(piece_of(own_ref, place, c), held[c].at[0], local_sem.at[c])
        for c in range(CHUNKS)
    ]
    own_rows = pl.ds(pl.multiple_of(group * shard_rows, shard_rows), shard_rows)
    own_shards = [
        pltpu.make_async_copy(
            shard_ref.at[kv, :, pl.ds(half * HALF, HALF)],
            prompt[half].at[kv, own_rows],
            local_sem.at[6 + 2 * half + kv],
        )
        for kv in range(2)
        for half in range(2)
    ]
    for copy in own_pieces + own_shards:
        copy.start()

    def outgoing(k, carry):
        base = ((group + k) % groups) * blocks

        def look(j, found):
            count, first, second = found
            parent = anc_ref[base + j]
            hit = (parent >> 5) == group
            slot = (parent - place) & (blocks - 1)
            first = jnp.where(hit & (count == 0), slot, first)
            second = jnp.where(hit & (count == 1), slot, second)
            return count + hit.astype(jnp.int32), first, second

        zero = jnp.int32(0)
        _, first, second = lax.fori_loop(0, blocks, look, (zero, zero, zero), unroll=8)
        out_tab[k * CAP] = first
        out_tab[k * CAP + 1] = second
        return carry

    lax.fori_loop(0, groups, outgoing, 0)

    def incoming(k, carry):
        j = (place + k) % blocks
        parent = anc_ref[group * blocks + j]
        source = parent >> 5

        def look(i, rank):
            same = ((anc_ref[group * blocks + i] >> 5) == source) & (i < j)
            return jnp.where(same, 1, rank)

        rank = lax.fori_loop(0, blocks, look, jnp.int32(0), unroll=8)
        slot = ((source - group) & (groups - 1)) * CAP + rank
        in_tab[k] = jnp.where(parent >= 0, slot, 0)
        return carry

    lax.fori_loop(0, blocks, incoming, 0)

    pl.semaphore_wait(barrier, blocks + groups - 2)

    def send_held(c):
        def step(k, carry):
            peer = (place + k) % blocks
            pltpu.make_async_remote_copy(
                src_ref=piece_of(own_ref, peer, c),
                dst_ref=held[c].at[blocks - k],
                send_sem=held_send.at[c],
                recv_sem=held_recv.at[c, blocks - k],
                device_id={"head": peer},
                device_id_type=MESH,
            ).start()
            return carry

        lax.fori_loop(1, blocks, step, 0)

    def shard_cols(half):
        return pl.ds(half * HALF, HALF)

    def send_shard(half):
        def step(k, carry):
            peer = (group + k) % groups
            pltpu.make_async_remote_copy(
                src_ref=shard_ref.at[core, :, shard_cols(half)],
                dst_ref=prompt[half].at[core, own_rows],
                send_sem=prompt_send.at[half],
                recv_sem=prompt_recv.at[half, groups - k],
                device_id={"seq": peer},
                device_id_type=MESH,
            ).start()
            return carry

        lax.fori_loop(1, groups, step, 0)

    def pass_shard(half):
        def step(k, carry):
            source = (group + k) % groups
            rows = pl.ds(pl.multiple_of(source * shard_rows, shard_rows), shard_rows)
            view = prompt[half].at[core, rows]
            pltpu.make_async_copy(view, view, prompt_recv.at[half, k]).wait()
            pltpu.make_async_remote_copy(
                src_ref=view,
                dst_ref=view,
                send_sem=pass_send.at[half],
                recv_sem=pass_recv.at[half, k],
                device_id={"head": twin},
                device_id_type=MESH,
            ).start()
            return carry

        lax.fori_loop(1, groups, step, 0)

    def wait_bytes(view, sem):
        pltpu.make_async_copy(view, view, sem).wait()

    def others(kv, half):
        return prompt[half].at[kv, pl.ds(0, prompt_rows - shard_rows)]

    def relay_groups(c):
        def arrive(k, carry):
            wait_bytes(held[c].at[k], held_recv.at[c, k])
            return carry

        lax.fori_loop(1, blocks, arrive, 0)
        own_pieces[c].wait()

        def pick(i, carry):
            sent[c][i] = held[c][out_tab[i]]
            return carry

        lax.fori_loop(0, groups * CAP, pick, 0)
        here = pltpu.make_async_copy(
            sent[c].at[pl.ds(0, CAP)], landed[c].at[pl.ds(0, CAP)], local_sem.at[4 + c]
        )
        here.start()

        def step(k, carry):
            pltpu.make_async_remote_copy(
                src_ref=sent[c].at[pl.ds(k * CAP, CAP)],
                dst_ref=landed[c].at[pl.ds((groups - k) * CAP, CAP)],
                send_sem=land_send.at[c],
                recv_sem=land_recv.at[c, groups - k],
                device_id={"seq": (group + k) % groups},
                device_id_type=MESH,
            ).start()
            return carry

        lax.fori_loop(1, groups, step, 0)
        here.wait()

    def relay_blocks(c):
        def arrive(k, carry):
            wait_bytes(landed[c].at[pl.ds(k * CAP, CAP)], land_recv.at[c, k])
            return carry

        lax.fori_loop(1, groups, arrive, 0)

        def pick(i, carry):
            spread[c][i] = landed[c][in_tab[i]]
            return carry

        lax.fori_loop(0, blocks, pick, 0)
        here = pltpu.make_async_copy(spread[c].at[0], far[c].at[place], local_sem.at[2 + c])
        here.start()

        def step(k, carry):
            pltpu.make_async_remote_copy(
                src_ref=spread[c].at[k],
                dst_ref=far[c].at[place],
                send_sem=far_send.at[c],
                recv_sem=far_recv.at[c, blocks - k],
                device_id={"head": (place + k) % blocks},
                device_id_type=MESH,
            ).start()
            return carry

        lax.fori_loop(1, blocks, step, 0)
        here.wait()

    near = prompt_rows + BLOCK
    rows = HEADS * BLOCK
    row = lax.broadcasted_iota(jnp.int32, (rows, BLOCK), 0) % BLOCK
    col = lax.broadcasted_iota(jnp.int32, (rows, BLOCK), 1)
    causal = col <= row
    v_s[:, HEAD_SIZE:] = jnp.ones((near, HEAD_SIZE), jnp.bfloat16)
    ones = jnp.ones((BLOCK, HEAD_SIZE), jnp.bfloat16)
    has_parent = anc_ref[group * blocks + place] >= 0

    def spans(head, step):
        return [
            pl.ds(
                pl.multiple_of(head * (RATIO * HEAD_SIZE), HEAD_SIZE)
                + (step * HEADS + i) * HEAD_SIZE,
                HEAD_SIZE,
            )
            for i in range(HEADS)
        ]

    def head_cols(head):
        return pl.ds(pl.multiple_of(head * HEAD_SIZE, HEAD_SIZE), HEAD_SIZE)

    def attend_near(half, place_in_half):
        head = half * (KEY_VALUE_HEADS // 2) + place_in_half
        for target, kv in ((k_s, 0), (v_s, 1)):
            target[0:prompt_rows, 0:HEAD_SIZE] = prompt[half][kv, :, head_cols(place_in_half)]
            target[prompt_rows:near, 0:HEAD_SIZE] = own_ref[kv, :, head_cols(head)]
        for step in range(RATIO // HEADS):
            q = jnp.concatenate([q_ref[:, span] for span in spans(head, step)], axis=0)
            scores = dot(q, k_s[...], 1)
            own = jnp.where(causal, scores[:, prompt_rows:], -jnp.inf)
            scores = jnp.concatenate([scores[:, :prompt_rows], own], axis=1)
            peak = jnp.max(scores, axis=1, keepdims=True)
            weights = jnp.exp2(scores * EXP2_SCALE - peak * EXP2_SCALE)
            acc_s[head, step * rows : (step + 1) * rows] = dot(
                weights.astype(jnp.bfloat16), v_s[...], 0
            )
            peak_s[head, step * rows : (step + 1) * rows] = jnp.broadcast_to(
                peak, (rows, HEAD_SIZE)
            )

    def attend_far(c, side, place_in_chunk):
        head = side * (KEY_VALUE_HEADS // 2) + c * 2 + place_in_chunk
        bands = BLOCK // PIECE_ROWS

        def load(kv):
            return jnp.concatenate(
                [
                    far[c][(kv * bands + band) * 2 + side, :, head_cols(place_in_chunk)]
                    for band in range(bands)
                ],
                axis=0,
            )

        keys = load(0)
        values = jnp.concatenate([load(1), ones], axis=1)
        for step in range(RATIO // HEADS):
            here = spans(head, step)
            q = jnp.concatenate([q_ref[:, span] for span in here], axis=0)
            scores = jnp.where(has_parent, dot(q, keys, 1), -jnp.inf)
            before = peak_s[head, step * rows : (step + 1) * rows]
            peak = jnp.maximum(jnp.max(scores, axis=1, keepdims=True), before)
            weights = jnp.exp2((scores - peak) * EXP2_SCALE)
            scale = jnp.exp2((before - peak) * EXP2_SCALE)
            far_sum = dot(weights.astype(jnp.bfloat16), values, 0)
            near_sum = acc_s[head, step * rows : (step + 1) * rows]
            total = near_sum[:, :HEAD_SIZE] * scale + far_sum[:, :HEAD_SIZE]
            norm = near_sum[:, HEAD_SIZE:] * scale + far_sum[:, HEAD_SIZE:]
            out = (total / norm).astype(jnp.bfloat16)
            for i, span in enumerate(here):
                o_ref[:, span] = out[i * BLOCK : (i + 1) * BLOCK]

    def attend(half, first, last):
        def step(i, carry):
            attend_near(half, i)
            return carry

        lax.fori_loop(first, last, step, 0)

    def wait_half(half):
        pass_shard(half)

        def step(k, carry):
            source = (group + k) % groups
            rows = pl.ds(pl.multiple_of(source * shard_rows, shard_rows), shard_rows)
            wait_bytes(prompt[half].at[1 - core, rows], pass_recv.at[half, k])
            return carry

        lax.fori_loop(1, groups, step, 0)

    send_held(0)
    send_shard(0)
    send_held(1)
    send_shard(1)
    for copy in own_shards:
        copy.wait()

    wait_half(0)
    attend(0, 0, 1)
    relay_groups(0)
    attend(0, 1, 3)
    relay_blocks(0)
    attend(0, 3, 4)
    relay_groups(1)
    wait_half(1)
    attend(1, 0, 3)
    relay_blocks(1)
    attend(1, 3, 4)

    for c in range(CHUNKS):
        view = held[c].at[pl.ds(1, blocks - 1)]

        def arrive(k, carry):
            wait_bytes(far[c].at[(place + k) % blocks], far_recv.at[c, k])
            return carry

        lax.fori_loop(1, blocks, arrive, 0)

        def step(i, carry):
            attend_far(c, i // 2, i % 2)
            return carry

        lax.fori_loop(0, KEY_VALUE_HEADS // CHUNKS, step, 0)
        wait_bytes(view, held_send.at[c])
        wait_bytes(sent[c].at[pl.ds(CAP, (groups - 1) * CAP)], land_send.at[c])
        wait_bytes(view, far_send.at[c])
    for half in range(2):
        wait_bytes(others(core, half), prompt_send.at[half])
        wait_bytes(others(core, half), pass_send.at[half])


def body(query, sampled_key_value, cached_prompt_key_value, ancestor_block):
    groups = lax.axis_size("seq")
    blocks = lax.axis_size("head")
    prompt_rows = groups * cached_prompt_key_value.shape[1]
    near = prompt_rows + BLOCK
    bf16 = jnp.bfloat16
    vmem = pl.BlockSpec(memory_space=pltpu.VMEM)
    dma = pltpu.SemaphoreType.DMA
    return pl.pallas_call(
        functools.partial(kernel, groups, blocks),
        in_specs=[pl.BlockSpec(memory_space=pltpu.SMEM), vmem, vmem, vmem],
        out_specs=vmem,
        out_shape=jax.ShapeDtypeStruct(query.shape, query.dtype),
        scratch_shapes=[
            *[pltpu.VMEM((2, prompt_rows, HALF), bf16)] * 2,
            *[pltpu.VMEM((blocks, PIECE_ROWS, CHUNK_COLS), bf16)] * CHUNKS,
            *[pltpu.VMEM((groups * CAP, PIECE_ROWS, CHUNK_COLS), bf16)] * (2 * CHUNKS),
            *[pltpu.VMEM((blocks, PIECE_ROWS, CHUNK_COLS), bf16)] * CHUNKS,
            *[pltpu.VMEM((blocks, PIECE_ROWS, CHUNK_COLS), bf16)] * CHUNKS,
            pltpu.VMEM((near, HEAD_SIZE), bf16),
            pltpu.VMEM((near, 2 * HEAD_SIZE), bf16),
            pltpu.VMEM((KEY_VALUE_HEADS, RATIO * BLOCK, 2 * HEAD_SIZE), jnp.float32),
            pltpu.VMEM((KEY_VALUE_HEADS, RATIO * BLOCK, HEAD_SIZE), jnp.float32),
            pltpu.SMEM((groups * CAP,), jnp.int32),
            pltpu.SMEM((blocks,), jnp.int32),
            dma((CHUNKS,)),
            dma((CHUNKS, blocks)),
            dma((CHUNKS,)),
            dma((CHUNKS, groups)),
            dma((CHUNKS,)),
            dma((CHUNKS, blocks)),
            dma((2,)),
            dma((2, groups)),
            dma((2,)),
            dma((2, groups)),
            dma((10,)),
        ],
        compiler_params=pltpu.CompilerParams(
            collective_id=0, has_side_effects=True, vmem_limit_bytes=60 * 2**20
        ),
        name="tree_attention",
    )(ancestor_block, query, sampled_key_value, cached_prompt_key_value)


def solution(mesh):
    placed = (P(("seq", "head"), None), P(None, ("seq", "head"), None), P(None, "seq", None), P())
    return jax.shard_map(
        body, mesh=mesh, in_specs=placed, out_specs=P(("seq", "head"), None), check_vma=False
    )
```

```python
import functools
import math

import jax
import jax.numpy as jnp
from jax import lax
from jax.experimental import pallas as pl
from jax.experimental.pallas import tpu as pltpu
from jax.sharding import PartitionSpec as P

QUERY_HEADS = 64
KEY_VALUE_HEADS = 8
HEAD_SIZE = 128
BLOCK = 128
RATIO = QUERY_HEADS // KEY_VALUE_HEADS
CAP = 2
WIDTH = KEY_VALUE_HEADS * HEAD_SIZE
PIECE_ROWS = 16
PIECE_COLS = WIDTH // 2
CHUNKS = 2
CHUNK_COLS = PIECE_COLS // CHUNKS
PARTS = 4
PART_HEADS = KEY_VALUE_HEADS // PARTS
PART_COLS = WIDTH // PARTS
HEADS = 2
EXP2_SCALE = math.log2(math.e) / math.sqrt(HEAD_SIZE)
MESH = pl.DeviceIdType.MESH


def dot(left, right, contract_right):
    return lax.dot_general(
        left, right, (((1,), (contract_right,)), ((), ())), preferred_element_type=jnp.float32
    )


def piece_of(ref, index, chunk):
    row = pl.multiple_of(((index // 2) % (BLOCK // PIECE_ROWS)) * PIECE_ROWS, PIECE_ROWS)
    col = pl.multiple_of((index % 2) * PIECE_COLS + chunk * CHUNK_COLS, CHUNK_COLS)
    kv = index // (2 * (BLOCK // PIECE_ROWS))
    return ref.at[kv, pl.ds(row, PIECE_ROWS), pl.ds(col, CHUNK_COLS)]


def kernel(
    groups,
    blocks,
    anc_ref,
    q_ref,
    own_ref,
    shard_ref,
    o_ref,
    prompt_0,
    prompt_1,
    prompt_2,
    prompt_3,
    held_0,
    held_1,
    sent_0,
    sent_1,
    landed_0,
    landed_1,
    spread_0,
    spread_1,
    far_0,
    far_1,
    k_s,
    v_s,
    acc_s,
    peak_s,
    out_tab,
    in_tab,
    held_send,
    held_recv,
    land_send,
    land_recv,
    far_send,
    far_recv,
    prompt_send,
    prompt_recv,
    pass_send,
    pass_recv,
    local_sem,
):
    held, sent = (held_0, held_1), (sent_0, sent_1)
    landed, spread = (landed_0, landed_1), (spread_0, spread_1)
    prompt, far = (prompt_0, prompt_1, prompt_2, prompt_3), (far_0, far_1)
    group = lax.axis_index("seq")
    place = lax.axis_index("head")
    core = place % 2
    twin = place + 1 - 2 * core
    shard_rows = shard_ref.shape[1]
    prompt_rows = groups * shard_rows

    barrier = pltpu.get_barrier_semaphore()

    def greet(axis, size, me):
        def step(k, carry):
            pl.semaphore_signal(
                barrier, inc=1, device_id={axis: (me + k) % size}, device_id_type=MESH
            )
            return carry

        lax.fori_loop(1, size, step, 0)

    greet("head", blocks, place)
    greet("seq", groups, group)

    own_pieces = [
        pltpu.make_async_copy(piece_of(own_ref, place, c), held[c].at[0], local_sem.at[c])
        for c in range(CHUNKS)
    ]
    own_rows = pl.ds(pl.multiple_of(group * shard_rows, shard_rows), shard_rows)
    own_shards = [
        pltpu.make_async_copy(
            shard_ref.at[kv, :, pl.ds(part * PART_COLS, PART_COLS)],
            prompt[part].at[kv, own_rows],
            local_sem.at[6 + 2 * part + kv],
        )
        for kv in range(2)
        for part in range(PARTS)
    ]
    for copy in own_pieces + own_shards:
        copy.start()

    pl.semaphore_wait(barrier, blocks + groups - 2)

    def farthest_first(send):
        def step(i, carry):
            send(blocks // 2 - i)
            send(blocks // 2 + 1 + i)
            return carry

        lax.fori_loop(0, blocks // 2 - 1, step, 0)
        send(1)

    def send_held(c):
        def send(k):
            peer = (place + k) % blocks
            pltpu.make_async_remote_copy(
                src_ref=piece_of(own_ref, peer, c),
                dst_ref=held[c].at[blocks - k],
                send_sem=held_send.at[c],
                recv_sem=held_recv.at[c, blocks - k],
                device_id={"head": peer},
                device_id_type=MESH,
            ).start()

        farthest_first(send)

    def shard_cols(part):
        return pl.ds(part * PART_COLS, PART_COLS)

    def send_shard(part):
        def step(k, carry):
            peer = (group + k) % groups
            pltpu.make_async_remote_copy(
                src_ref=shard_ref.at[core, :, shard_cols(part)],
                dst_ref=prompt[part].at[core, own_rows],
                send_sem=prompt_send.at[part],
                recv_sem=prompt_recv.at[part, groups - k],
                device_id={"seq": peer},
                device_id_type=MESH,
            ).start()
            return carry

        lax.fori_loop(1, groups, step, 0)

    def pass_shard(part):
        def step(k, carry):
            source = (group + k) % groups
            rows = pl.ds(pl.multiple_of(source * shard_rows, shard_rows), shard_rows)
            view = prompt[part].at[core, rows]
            pltpu.make_async_copy(view, view, prompt_recv.at[part, k]).wait()
            pltpu.make_async_remote_copy(
                src_ref=view,
                dst_ref=view,
                send_sem=pass_send.at[part],
                recv_sem=pass_recv.at[part, k],
                device_id={"head": twin},
                device_id_type=MESH,
            ).start()
            return carry

        lax.fori_loop(1, groups, step, 0)

    def wait_bytes(view, sem):
        pltpu.make_async_copy(view, view, sem).wait()

    def others(kv, part):
        return prompt[part].at[kv, pl.ds(0, prompt_rows - shard_rows)]

    def relay_groups(c):
        def arrive(k, carry):
            wait_bytes(held[c].at[k], held_recv.at[c, k])
            return carry

        lax.fori_loop(1, blocks, arrive, 0)
        own_pieces[c].wait()

        def pick(i, carry):
            sent[c][i] = held[c][out_tab[i]]
            return carry

        lax.fori_loop(0, groups * CAP, pick, 0)
        here = pltpu.make_async_copy(
            sent[c].at[pl.ds(0, CAP)], landed[c].at[pl.ds(0, CAP)], local_sem.at[4 + c]
        )
        here.start()

        def step(k, carry):
            pltpu.make_async_remote_copy(
                src_ref=sent[c].at[pl.ds(k * CAP, CAP)],
                dst_ref=landed[c].at[pl.ds((groups - k) * CAP, CAP)],
                send_sem=land_send.at[c],
                recv_sem=land_recv.at[c, groups - k],
                device_id={"seq": (group + k) % groups},
                device_id_type=MESH,
            ).start()
            return carry

        lax.fori_loop(1, groups, step, 0)
        here.wait()

    def relay_blocks(c):
        def arrive(k, carry):
            wait_bytes(landed[c].at[pl.ds(k * CAP, CAP)], land_recv.at[c, k])
            return carry

        lax.fori_loop(1, groups, arrive, 0)

        def pick(i, carry):
            spread[c][i] = landed[c][in_tab[i]]
            return carry

        lax.fori_loop(0, blocks, pick, 0)
        here = pltpu.make_async_copy(spread[c].at[0], far[c].at[place], local_sem.at[2 + c])
        here.start()

        def send(k):
            pltpu.make_async_remote_copy(
                src_ref=spread[c].at[k],
                dst_ref=far[c].at[place],
                send_sem=far_send.at[c],
                recv_sem=far_recv.at[c, blocks - k],
                device_id={"head": (place + k) % blocks},
                device_id_type=MESH,
            ).start()

        farthest_first(send)
        here.wait()

    near = prompt_rows + BLOCK
    rows = HEADS * BLOCK
    row = lax.broadcasted_iota(jnp.int32, (rows, BLOCK), 0) % BLOCK
    col = lax.broadcasted_iota(jnp.int32, (rows, BLOCK), 1)
    causal = col <= row
    v_s[:, HEAD_SIZE:] = jnp.ones((near, HEAD_SIZE), jnp.bfloat16)
    ones = jnp.ones((BLOCK, HEAD_SIZE), jnp.bfloat16)
    has_parent = anc_ref[group * blocks + place] >= 0

    def spans(head, step):
        return [
            pl.ds(
                pl.multiple_of(head * (RATIO * HEAD_SIZE), HEAD_SIZE)
                + (step * HEADS + i) * HEAD_SIZE,
                HEAD_SIZE,
            )
            for i in range(HEADS)
        ]

    def head_cols(head):
        return pl.ds(pl.multiple_of(head * HEAD_SIZE, HEAD_SIZE), HEAD_SIZE)

    def attend_near(part, place_in_part):
        head = part * PART_HEADS + place_in_part
        for target, kv in ((k_s, 0), (v_s, 1)):
            target[0:prompt_rows, 0:HEAD_SIZE] = prompt[part][kv, :, head_cols(place_in_part)]
            target[prompt_rows:near, 0:HEAD_SIZE] = own_ref[kv, :, head_cols(head)]
        for step in range(RATIO // HEADS):
            q = jnp.concatenate([q_ref[:, span] for span in spans(head, step)], axis=0)
            scores = dot(q, k_s[...], 1)
            own = jnp.where(causal, scores[:, prompt_rows:], -jnp.inf)
            scores = jnp.concatenate([scores[:, :prompt_rows], own], axis=1)
            peak = jnp.max(scores, axis=1, keepdims=True)
            weights = jnp.exp2(scores * EXP2_SCALE - peak * EXP2_SCALE)
            acc_s[head, step * rows : (step + 1) * rows] = dot(
                weights.astype(jnp.bfloat16), v_s[...], 0
            )
            peak_s[head, step * rows : (step + 1) * rows] = jnp.broadcast_to(
                peak, (rows, HEAD_SIZE)
            )

    def attend_far(c, side, place_in_chunk):
        head = side * (KEY_VALUE_HEADS // 2) + c * 2 + place_in_chunk
        bands = BLOCK // PIECE_ROWS

        def load(kv):
            return jnp.concatenate(
                [
                    far[c][(kv * bands + band) * 2 + side, :, head_cols(place_in_chunk)]
                    for band in range(bands)
                ],
                axis=0,
            )

        keys = load(0)
        values = jnp.concatenate([load(1), ones], axis=1)
        for step in range(RATIO // HEADS):
            here = spans(head, step)
            q = jnp.concatenate([q_ref[:, span] for span in here], axis=0)
            scores = jnp.where(has_parent, dot(q, keys, 1), -jnp.inf)
            before = peak_s[head, step * rows : (step + 1) * rows]
            peak = jnp.maximum(jnp.max(scores, axis=1, keepdims=True), before)
            weights = jnp.exp2((scores - peak) * EXP2_SCALE)
            scale = jnp.exp2((before - peak) * EXP2_SCALE)
            far_sum = dot(weights.astype(jnp.bfloat16), values, 0)
            near_sum = acc_s[head, step * rows : (step + 1) * rows]
            total = near_sum[:, :HEAD_SIZE] * scale + far_sum[:, :HEAD_SIZE]
            norm = near_sum[:, HEAD_SIZE:] * scale + far_sum[:, HEAD_SIZE:]
            out = (total / norm).astype(jnp.bfloat16)
            for i, span in enumerate(here):
                o_ref[:, span] = out[i * BLOCK : (i + 1) * BLOCK]

    def attend(part):
        def step(i, carry):
            attend_near(part, i)
            return carry

        lax.fori_loop(0, PART_HEADS, step, 0)

    def wait_part(part):
        pass_shard(part)

        def step(k, carry):
            source = (group + k) % groups
            rows = pl.ds(pl.multiple_of(source * shard_rows, shard_rows), shard_rows)
            wait_bytes(prompt[part].at[1 - core, rows], pass_recv.at[part, k])
            return carry

        lax.fori_loop(1, groups, step, 0)

    send_held(0)
    send_shard(0)
    send_held(1)
    send_shard(1)

    def outgoing(k, carry):
        base = ((group + k) % groups) * blocks

        def look(j, found):
            count, first, second = found
            parent = anc_ref[base + j]
            hit = (parent >> 5) == group
            slot = (parent - place) & (blocks - 1)
            first = jnp.where(hit & (count == 0), slot, first)
            second = jnp.where(hit & (count == 1), slot, second)
            return count + hit.astype(jnp.int32), first, second

        zero = jnp.int32(0)
        _, first, second = lax.fori_loop(0, blocks, look, (zero, zero, zero), unroll=8)
        out_tab[k * CAP] = first
        out_tab[k * CAP + 1] = second
        return carry

    lax.fori_loop(0, groups, outgoing, 0)

    def incoming(k, carry):
        j = (place + k) % blocks
        parent = anc_ref[group * blocks + j]
        source = parent >> 5

        def look(i, rank):
            same = ((anc_ref[group * blocks + i] >> 5) == source) & (i < j)
            return jnp.where(same, 1, rank)

        rank = lax.fori_loop(0, blocks, look, jnp.int32(0), unroll=8)
        slot = ((source - group) & (groups - 1)) * CAP + rank
        in_tab[k] = jnp.where(parent >= 0, slot, 0)
        return carry

    lax.fori_loop(0, blocks, incoming, 0)

    for copy in own_shards:
        copy.wait()

    wait_part(0)
    attend(0)
    relay_groups(0)
    send_shard(2)
    wait_part(1)
    attend(1)
    relay_blocks(0)
    relay_groups(1)
    send_shard(3)
    wait_part(2)
    attend(2)
    relay_blocks(1)
    wait_part(3)
    attend(3)

    for c in range(CHUNKS):
        view = held[c].at[pl.ds(1, blocks - 1)]

        def arrive(k, carry):
            wait_bytes(far[c].at[(place + k) % blocks], far_recv.at[c, k])
            return carry

        lax.fori_loop(1, blocks, arrive, 0)

        def step(i, carry):
            attend_far(c, i // 2, i % 2)
            return carry

        lax.fori_loop(0, KEY_VALUE_HEADS // CHUNKS, step, 0)
        wait_bytes(view, held_send.at[c])
        wait_bytes(sent[c].at[pl.ds(CAP, (groups - 1) * CAP)], land_send.at[c])
        wait_bytes(view, far_send.at[c])
    for part in range(PARTS):
        wait_bytes(others(core, part), prompt_send.at[part])
        wait_bytes(others(core, part), pass_send.at[part])


def body(query, sampled_key_value, cached_prompt_key_value, ancestor_block):
    groups = lax.axis_size("seq")
    blocks = lax.axis_size("head")
    prompt_rows = groups * cached_prompt_key_value.shape[1]
    near = prompt_rows + BLOCK
    bf16 = jnp.bfloat16
    vmem = pl.BlockSpec(memory_space=pltpu.VMEM)
    dma = pltpu.SemaphoreType.DMA
    return pl.pallas_call(
        functools.partial(kernel, groups, blocks),
        in_specs=[pl.BlockSpec(memory_space=pltpu.SMEM), vmem, vmem, vmem],
        out_specs=vmem,
        out_shape=jax.ShapeDtypeStruct(query.shape, query.dtype),
        scratch_shapes=[
            *[pltpu.VMEM((2, prompt_rows, PART_COLS), bf16)] * PARTS,
            *[pltpu.VMEM((blocks, PIECE_ROWS, CHUNK_COLS), bf16)] * CHUNKS,
            *[pltpu.VMEM((groups * CAP, PIECE_ROWS, CHUNK_COLS), bf16)] * (2 * CHUNKS),
            *[pltpu.VMEM((blocks, PIECE_ROWS, CHUNK_COLS), bf16)] * CHUNKS,
            *[pltpu.VMEM((blocks, PIECE_ROWS, CHUNK_COLS), bf16)] * CHUNKS,
            pltpu.VMEM((near, HEAD_SIZE), bf16),
            pltpu.VMEM((near, 2 * HEAD_SIZE), bf16),
            pltpu.VMEM((KEY_VALUE_HEADS, RATIO * BLOCK, 2 * HEAD_SIZE), jnp.float32),
            pltpu.VMEM((KEY_VALUE_HEADS, RATIO * BLOCK, HEAD_SIZE), jnp.float32),
            pltpu.SMEM((groups * CAP,), jnp.int32),
            pltpu.SMEM((blocks,), jnp.int32),
            dma((CHUNKS,)),
            dma((CHUNKS, blocks)),
            dma((CHUNKS,)),
            dma((CHUNKS, groups)),
            dma((CHUNKS,)),
            dma((CHUNKS, blocks)),
            dma((PARTS,)),
            dma((PARTS, groups)),
            dma((PARTS,)),
            dma((PARTS, groups)),
            dma((6 + 2 * PARTS,)),
        ],
        compiler_params=pltpu.CompilerParams(
            collective_id=0, has_side_effects=True, vmem_limit_bytes=30 * 2**20
        ),
        name="tree_attention",
    )(ancestor_block, query, sampled_key_value, cached_prompt_key_value)


def solution(mesh):
    placed = (P(("seq", "head"), None), P(None, ("seq", "head"), None), P(None, "seq", None), P())
    return jax.shard_map(
        body, mesh=mesh, in_specs=placed, out_specs=P(("seq", "head"), None), check_vma=False
    )
```
